32 devices in a mesh: col: 4 (over z), tok: 4 (over y, x), row: 2 (over core).
Axes of the slice: x: 2, y: 2, z: 4, core: 2. Of those that a mesh axis runs over, the one named last changes fastest.
Arguments:
- activations: bfloat16 [4096, 2048], P('tok', 'col'), may hold values from -40 to 40
- weight: bfloat16 [8192, 2048], P(('tok', 'row'), 'col'), may hold values from -6 to 6
- inverse_rows: float32 [512, 2048], P('tok', 'col'), may hold values from -1 to 2, as said below
- prune_masks: int32 [3, 2048], replicated, may hold values from 0 to 1, as said below
- panel_order: int32 [16], replicated, may hold values from 0 to 15, each once
Outputs:
- hessian_panel: float32 [512, 2048], P('tok', ('col', 'row'))
- pruned_weights: bfloat16 [3, 8192, 2048], P(None, ('tok', 'row'), 'col')
The draws below stay inside these ranges and needn't reach their ends.
Inputs may be any that keep to these rules, and one draw needn't show every extreme that they name: `inverse_rows`: in column panel c, the entry of row i and column c * 512 + i lies between 0.5 and 2. `prune_masks`: in every aligned block of 128 columns, level 0 marks exactly 64 columns, level 1 exactly 76, level 2 exactly 89. `panel_order`: the first entry names a mask block of the panel that is processed.
All inputs are finite; a program needn't handle non-finite values.
Results may differ from the reference program's by a relative error of at most 0.001.
Values may be sent and summed in bfloat16 or wider, within the bound.
No kernel may reach another device: no remote copies, remote signals or barrier semaphores. Data moves between devices by JAX's collectives and lax.ppermute only.
A program may use at most 64 MiB of HBM per device.

```python
import math
import jax
import jax.numpy as jnp
from jax import lax

COLB = 512
MB = 128
OUT = 8192
D = 2048
TOKENS = 4096


def draw_activations(key, part):
    key_list = jax.random.split(jax.random.fold_in(key, 11), 3)
    normal_part = jnp.clip(jax.random.normal(key_list[0], (TOKENS, D), jnp.float32), -6.0, 6.0)
    token_scale = jnp.exp(jax.random.uniform(key_list[1], (TOKENS, 1), jnp.float32, math.log(0.3), math.log(3.0)))
    column_scale = jnp.exp(jax.random.uniform(key_list[2], (1, D), jnp.float32, math.log(0.4), math.log(4.0)))
    return jnp.clip(0.5 * normal_part * token_scale * column_scale, -40.0, 40.0).astype(jnp.bfloat16)


def draw_inverse_rows(key, part):
    key_list = jax.random.split(jax.random.fold_in(key, 17), 2)
    spread = 0.6 / math.sqrt(COLB)
    off_part = jnp.clip(jax.random.normal(key_list[0], (COLB, D), jnp.float32), -4.0, 4.0) * spread
    diag_scale = jnp.exp(jax.random.uniform(key_list[1], (COLB, D // COLB), jnp.float32, math.log(0.5), math.log(2.0)))
    on_diagonal = (jnp.arange(COLB)[:, None] == jnp.arange(D)[None, :] % COLB).astype(jnp.float32)
    return off_part * (1.0 - on_diagonal) + on_diagonal * jnp.repeat(diag_scale, COLB, axis=1)


def draw_prune_masks(key, part):
    block_count = D // MB
    key_list = jax.random.split(jax.random.fold_in(key, 23), 3 * block_count)
    ranks = jax.vmap(lambda item_key: jax.random.permutation(item_key, MB))(key_list).reshape(3, D)
    counts = jnp.array([MB * 50 // 100, MB * 60 // 100, MB * 70 // 100], jnp.int32)
    return (ranks < counts[:, None]).astype(jnp.int32)


def level_of(own_key, shape, cuts, low, high):
    gain = 1.0
    for dim, shards_of in cuts:
        steps = jax.random.uniform(jax.random.fold_in(jax.random.fold_in(own_key, 6), dim), (shards_of,), jnp.float32, low / len(cuts), high / len(cuts))
        gain = gain * jnp.repeat(jnp.exp(steps), shape[dim] // shards_of).reshape((-1,) + (1,) * (len(shape) - 1 - dim))
    return gain


def bell_draw(stream_key, extent, scale, bound, cuts=(), held_as=jnp.bfloat16):
    entries = jax.random.normal(stream_key, extent, jnp.float32) * scale
    if len(cuts) > 0:
        entries = level_of(stream_key, extent, cuts, -0.22, 0.18) * entries
    return jnp.clip(entries, min=-bound, max=bound).astype(held_as)


def setup_inputs(seed: int = 0) -> dict:
    splits = jax.random.split(jax.random.key(seed), 6)
    return {
        "activations": draw_activations(jax.random.fold_in(splits[5], 71), 0),
        "weight": bell_draw(splits[1], (OUT, D), 1.0, 6.0, ((0, 8), (1, 4))),
        "inverse_rows": draw_inverse_rows(jax.random.fold_in(splits[5], 71), 0),
        "prune_masks": draw_prune_masks(jax.random.fold_in(splits[5], 71), 0),
        "panel_order": jax.random.permutation(splits[4], D // MB).astype(jnp.int32),
    }


def block_inverse(square):
    width = square.shape[0]
    scale = jnp.diagonal(square)
    identity = jnp.eye(width, dtype=square.dtype)
    negated = identity - square / scale[:, None]
    result = identity + negated
    reach = 2
    while reach < width:
        negated = jnp.dot(negated, negated, precision=lax.Precision.HIGHEST, preferred_element_type=jnp.float32)
        result = jnp.dot(result, identity + negated, precision=lax.Precision.HIGHEST, preferred_element_type=jnp.float32)
        reach = reach * 2
    return result / scale[None, :]


def solve_upper_right(system, target):
    width = system.shape[0]
    pieces = []
    for start in range(0, width, MB):
        rhs = target[:, start:start + MB]
        if pieces:
            done = jnp.concatenate(pieces, axis=1)
            rhs = rhs - jnp.dot(done, system[:start, start:start + MB], precision=lax.Precision.HIGHEST, preferred_element_type=jnp.float32)
        inverse = block_inverse(system[start:start + MB, start:start + MB])
        pieces.append(jnp.dot(rhs, inverse, precision=lax.Precision.HIGHEST, preferred_element_type=jnp.float32))
    return jnp.concatenate(pieces, axis=1)


def reference(activations, weight, inverse_rows, prune_masks, panel_order):
    panel_root = (panel_order[0] // (COLB // MB)).astype(jnp.int32)
    begin_col = (panel_root * COLB).astype(jnp.int32)
    panel_acts = lax.dynamic_slice_in_dim(activations, begin_col, COLB, 1)
    hessian_panel = jnp.dot(panel_acts.T, activations, preferred_element_type=jnp.float32) * (2.0 / TOKENS)
    diag_block = lax.dynamic_slice_in_dim(inverse_rows, begin_col, COLB, 1)
    upper_part = jnp.triu(diag_block)
    column_ids = jnp.arange(D, dtype=jnp.int32)
    in_panel = (column_ids // COLB) == panel_root
    below_diag = in_panel[None, :] & ((column_ids[None, :] - begin_col) < jnp.arange(COLB, dtype=jnp.int32)[:, None])
    applied = jnp.where(below_diag, jnp.zeros_like(inverse_rows), inverse_rows)
    level_masks = lax.dynamic_slice_in_dim(prune_masks, begin_col, COLB, 1).astype(jnp.float32)
    panel_rows = lax.dynamic_slice_in_dim(weight, begin_col, COLB, 1).astype(jnp.float32)
    full_rows = weight.astype(jnp.float32)

    def solve_level(pruned):
        system = upper_part * pruned[:, None] * pruned[None, :] + jnp.diag(1.0 - pruned)
        target = panel_rows * pruned[None, :]
        errors = solve_upper_right(system, target)
        change = jnp.dot(errors, applied, precision=lax.Precision.HIGHEST, preferred_element_type=jnp.float32)
        keep_mask = lax.dynamic_update_slice(jnp.ones((D,), jnp.float32), 1.0 - pruned, (begin_col,))
        return ((full_rows - change) * keep_mask[None, :]).astype(jnp.bfloat16)

    pruned_weights = lax.map(solve_level, level_masks)
    return hessian_panel, pruned_weights
```

```python
import jax
import jax.numpy as jnp
from jax import lax
from jax.experimental import pallas as pl
from jax.experimental.pallas import tpu as pltpu
from jax.sharding import PartitionSpec as P

MB = 128
CHUNK = 128
DELAY = 3
GROUP = 2
F32 = jnp.float32
BF16 = jnp.bfloat16


def split_pair(x):
    high = lax.reduce_precision(x, 8, 7)
    return high.astype(BF16), (x - high).astype(BF16)


def split_in_kernel(x):
    high = x.astype(BF16)
    return high, (x - high.astype(F32)).astype(BF16)


def mm(a, b):
    return jnp.dot(a, b, preferred_element_type=F32)


def mm3(a_high, a_low, b_high, b_low):
    return mm(a_high, b_high) + mm(a_high, b_low) + mm(a_low, b_high)


def ring_order(count):
    return [0] + list(range(1, count, 2)) + list(range((count - 1) // 2 * 2, 0, -2))


def factor_kernel(
    meta, mine_u, other_u, mine_f, other_f, prow, pcol, k_high, k_low,
    u_high, u_low, f_high, f_low, lhs_high, lhs_low, total,
    *, tok_count, rows, levels,
):
    tok, core, holds = meta[0], meta[1], meta[2]
    width = u_high.shape[0]
    half = rows // 2
    stride = mine_u.shape[0] // tok_count
    for hop in range(tok_count):
        source = lax.rem(tok + hop, tok_count) if tok_count & (tok_count - 1) else tok ^ hop
        for pieces, side in ((0, core), (1, 1 - core)):
            at = pl.ds(pl.multiple_of(source * rows + side * half, half), half)
            u_ref = (mine_u, other_u)[pieces]
            f_ref = (mine_f, other_f)[pieces]
            top = hop * stride
            u_high[at, :] = u_ref[top : top + half, :]
            u_low[at, :] = u_ref[top + half : top + 2 * half, :]
            f_high[at, :] = f_ref[top : top + half, :]
            f_low[at, :] = f_ref[top + half : top + 2 * half, :]

    blocks = width // MB
    row_ids = lax.broadcasted_iota(jnp.int32, (MB, MB), 0)
    col_ids = lax.broadcasted_iota(jnp.int32, (MB, MB), 1)
    eye = jnp.where(row_ids == col_ids, 1.0, 0.0).astype(F32)
    ratio = []
    for blk in range(blocks):
        span = slice(blk * MB, (blk + 1) * MB)
        square = u_high[span, span].astype(F32) + u_low[span, span].astype(F32)
        diag = jnp.sum(square * eye, axis=1, keepdims=True)
        inverse = 1.0 / diag
        strict = jnp.where(col_ids > row_ids, square, 0.0)
        ratio.append([])
        for lvl in range(levels):
            share = pcol[span, lvl : lvl + 1] * inverse
            ratio[blk].append(share)
            negated = -(strict * share) * prow[lvl : lvl + 1, span]
            high, low = split_in_kernel(negated)
            at = blk * levels + lvl
            lhs_high[at, :MB] = high
            lhs_low[at, :MB] = low
            lhs_high[at, MB:] = eye.astype(BF16)
            lhs_low[at, MB:] = jnp.zeros((MB, MB), BF16)
            total[at] = eye

    def double(step, carry):
        for at in range(blocks * levels):
            power = lhs_high[at, :MB]
            both = jnp.concatenate([power, lhs_low[at, :MB]], axis=1)
            first = mm(lhs_high[at], both)
            second = mm(lhs_low[at], power)
            joined = first[:, :MB] + first[:, MB:] + second
            grown = total[at] + joined[MB:]
            total[at] = grown
            high, low = split_in_kernel(joined[:MB])
            lhs_high[at, :MB] = high
            lhs_low[at, :MB] = low
            high, low = split_in_kernel(grown)
            lhs_high[at, MB:] = high
            lhs_low[at, MB:] = low
        return carry

    lax.fori_loop(0, MB.bit_length() - 1, double, 0)

    cols = f_high.shape[1]
    for blk in reversed(range(blocks)):
        span = slice(blk * MB, (blk + 1) * MB)
        rest = slice((blk + 1) * MB, width)
        applied = f_high[span, :].astype(F32) + f_low[span, :].astype(F32)
        below = lax.broadcasted_iota(jnp.int32, (MB, cols), 1) < (
            lax.broadcasted_iota(jnp.int32, (MB, cols), 0) + blk * MB
        )
        applied = jnp.where(jnp.logical_and(below, holds == 1), 0.0, applied)
        for lvl in range(levels):
            lanes = slice(lvl * cols, (lvl + 1) * cols)
            target = applied
            if blk < blocks - 1:
                target = target - mm3(
                    u_high[span, rest], u_low[span, rest], k_high[rest, lanes], k_low[rest, lanes]
                )
            target = target * ratio[blk][lvl]
            high, low = split_in_kernel(target)
            at = blk * levels + lvl
            solved = mm3(lhs_high[at, MB:], lhs_low[at, MB:], high, low)
            high, low = split_in_kernel(solved)
            k_high[span, lanes] = high
            k_low[span, lanes] = low


def factor_call(meta, mine_u, other_u, mine_f, other_f, prow, pcol, tok_count, rows):
    levels, width = prow.shape
    cols = mine_f.shape[1]
    systems = width // MB * levels
    vmem = pl.BlockSpec(memory_space=pltpu.VMEM)

    def kernel(*refs):
        factor_kernel(*refs, tok_count=tok_count, rows=rows, levels=levels)

    return pl.pallas_call(
        kernel,
        out_shape=[jax.ShapeDtypeStruct((width, levels * cols), BF16)] * 2,
        in_specs=[pl.BlockSpec(memory_space=pltpu.SMEM)] + [vmem] * 6,
        out_specs=[vmem] * 2,
        scratch_shapes=[
            pltpu.VMEM((width, width), BF16),
            pltpu.VMEM((width, width), BF16),
            pltpu.VMEM((width, cols), BF16),
            pltpu.VMEM((width, cols), BF16),
            pltpu.VMEM((systems, 2 * MB, MB), BF16),
            pltpu.VMEM((systems, 2 * MB, MB), BF16),
            pltpu.VMEM((systems, MB, MB), F32),
        ],
        compiler_params=pltpu.CompilerParams(vmem_limit_bytes=24 << 20),
        cost_estimate=pl.CostEstimate(
            flops=8_000_000_000, bytes_accessed=8 << 20, transcendentals=0
        ),
        name="factor",
    )(meta, mine_u, other_u, mine_f, other_f, prow, pcol)


def update_call(meta, options, weight, k_high, k_low, keep, result, group):
    levels, cols = keep.shape
    out_rows = weight.shape[0]
    count, hops = len(options), len(options[0])
    chunk, width = options[0][0].shape
    vmem = pl.BlockSpec(memory_space=pltpu.VMEM)

    def kernel(meta_ref, *refs):
        pieces = refs[: count * hops]
        w_ref, high_ref, low_ref, keep_ref = refs[count * hops : count * hops + 4]
        out_ref, picked = refs[-2], refs[-1]
        distance = meta_ref[3]
        for i in range(count):
            for j in range(hops):

                @pl.when(distance == j)
                def _():
                    picked[i * chunk : (i + 1) * chunk, :] = pieces[i * hops + j][...]

        panel = picked[...]
        for lvl in range(levels):
            lanes = slice(lvl * cols, (lvl + 1) * cols)
            change = mm(panel, high_ref[:, lanes]) + mm(panel, low_ref[:, lanes])
            value = (w_ref[...].astype(F32) - change) * keep_ref[lvl : lvl + 1, :]
            out_ref[lvl] = value.astype(BF16)

    tall = count * chunk
    operands = [meta] + [piece for item in options for piece in item] + [weight, k_high, k_low, keep]
    in_specs = [pl.BlockSpec(memory_space=pltpu.SMEM)] + [vmem] * (count * hops)
    in_specs += [pl.BlockSpec((tall, cols), lambda i: (group, 0))] + [vmem] * 3
    aliases = {}
    if result is not None:
        aliases = {len(operands): 0}
        operands.append(result)
        in_specs.append(pl.BlockSpec(memory_space=pl.ANY))
    return pl.pallas_call(
        kernel,
        grid=(1,),
        out_shape=jax.ShapeDtypeStruct((levels, out_rows, cols), BF16),
        in_specs=in_specs,
        out_specs=pl.BlockSpec((levels, tall, cols), lambda i: (0, group, 0)),
        scratch_shapes=[pltpu.VMEM((tall, width), BF16)],
        input_output_aliases=aliases,
        compiler_params=pltpu.CompilerParams(vmem_limit_bytes=16 << 20),
        cost_estimate=pl.CostEstimate(
            flops=4 * tall * width * levels * cols, bytes_accessed=4 << 20, transcendentals=0
        ),
        name="update",
    )(*operands)


def on_device(activations, weight, inverse_rows, prune_masks, panel_order):
    col_count = lax.axis_size("col")
    tok_count = lax.axis_size("tok")
    row_count = lax.axis_size("row")
    tok_rows, block_width = activations.shape
    out_rows = weight.shape[0]
    factor_rows = inverse_rows.shape[0]
    root = panel_order[0] // (block_width // MB)
    col, tok, core = lax.axis_index("col"), lax.axis_index("tok"), lax.axis_index("row")

    order = ring_order(col_count)
    ring = [(order[i], order[(i + 1) % col_count]) for i in range(col_count)]
    place = [order.index(i) for i in range(col_count)]
    spot = jnp.array(place, jnp.int32)
    distance = lax.rem(spot[col] - spot[root] + col_count, col_count)
    holds = (col == root).astype(jnp.int32)
    meta = jnp.stack([tok, core, holds, distance]).astype(jnp.int32)

    def tok_pairs(hop):
        if tok_count & (tok_count - 1):
            return [((i + hop) % tok_count, i) for i in range(tok_count)]
        return [(i ^ hop, i) for i in range(tok_count)]

    def tok_target(hop):
        if tok_count & (tok_count - 1):
            return lax.rem(tok - hop + tok_count, tok_count)
        return tok ^ hop

    swap = [(0, 1), (1, 0)]

    half = factor_rows // row_count
    own_half = lax.dynamic_slice_in_dim(inverse_rows, core * half, half, 0)
    own_piece = jnp.concatenate(split_pair(own_half), axis=0)
    piece_rows = own_piece.shape[0]
    if piece_rows < CHUNK:
        piece = jnp.pad(own_piece, ((0, CHUNK - piece_rows), (0, 0)))
    else:
        piece = own_piece
    core_rows = tok_rows // row_count
    core_acts = lax.dynamic_slice_in_dim(activations, core * core_rows, core_rows, 0)
    acts_chunks = core_rows // CHUNK
    weight_chunks = out_rows // CHUNK
    chunks = [piece]
    chunks += [core_acts[i * CHUNK : (i + 1) * CHUNK] for i in range(acts_chunks)]
    chunks += [weight[i * CHUNK : (i + 1) * CHUNK] for i in range(weight_chunks)]

    got = []
    for k in range(len(chunks) + DELAY * (col_count - 2)):
        send = chunks[k] if k < len(chunks) else None
        if k >= DELAY:
            send = got[k - DELAY] if send is None else jnp.where(distance == 0, send, got[k - DELAY])
        got.append(lax.ppermute(send, "col", ring))

    def places_of(index):
        return [chunks[index]] + [got[index + DELAY * (j - 1)] for j in range(1, col_count)]

    def pick(index):
        options = places_of(index)
        out = options[0]
        for j in range(1, col_count):
            out = jnp.where(distance == j, options[j], out)
        return out

    def gather(item):
        parts = [item] + [lax.ppermute(item, "tok", tok_pairs(hop)) for hop in range(1, tok_count)]
        mine = jnp.concatenate(parts, axis=0)
        return mine, lax.ppermute(mine, "row", swap)

    mine_f, other_f = gather(own_piece)
    mine_u, other_u = gather(pick(0)[:piece_rows])

    level_masks = lax.dynamic_slice_in_dim(
        prune_masks, root * block_width, block_width, 1
    ).astype(F32)
    k_high, k_low = factor_call(
        meta, mine_u, other_u, mine_f, other_f, level_masks, level_masks.T, tok_count, factor_rows
    )

    panel_acts = jnp.concatenate([pick(1 + i) for i in range(acts_chunks)], axis=0)
    norm_scale = 2.0 / (tok_rows * tok_count)
    product = lax.dot_general(
        panel_acts, core_acts, (((0,), (0,)), ((), ())), preferred_element_type=F32
    ) * norm_scale
    half_width = block_width // row_count
    kept = lax.dynamic_slice_in_dim(product, core * half_width, half_width, 1)
    given = lax.dynamic_slice_in_dim(product, (1 - core) * half_width, half_width, 1)
    kept = kept + lax.ppermute(given, "row", swap)
    hessian = lax.dynamic_slice_in_dim(kept, tok * factor_rows, factor_rows, 0)
    for hop in range(1, tok_count):
        part = lax.dynamic_slice_in_dim(kept, tok_target(hop) * factor_rows, factor_rows, 0)
        hessian = hessian + lax.ppermute(
            part, "tok", [(b, a) for a, b in tok_pairs(hop)] if tok_count & (tok_count - 1) == 0
            else [(i, (i - hop) % tok_count) for i in range(tok_count)]
        )

    keep = jnp.where(holds == 1, 1.0 - level_masks, jnp.ones_like(level_masks))
    result = None
    base = 1 + acts_chunks
    for group in range(weight_chunks // GROUP):
        options = [places_of(base + group * GROUP + i) for i in range(GROUP)]
        result = update_call(meta, options, weight, k_high, k_low, keep, result, group)
    return hessian, result


def solution(mesh):
    in_specs = (P("tok", "col"), P(("tok", "row"), "col"), P("tok", "col"), P(), P())
    out_specs = (P("tok", ("col", "row")), P(None, ("tok", "row"), "col"))
    return jax.shard_map(
        on_device, mesh=mesh, in_specs=in_specs, out_specs=out_specs, check_vma=False
    )
```

```python
import jax
import jax.numpy as jnp
from jax import lax
from jax.experimental import pallas as pl
from jax.experimental.pallas import tpu as pltpu
from jax.sharding import PartitionSpec as P

MB = 128
CHUNKS = 8
DELAY = 2
LAST = 2
F32 = jnp.float32
BF16 = jnp.bfloat16
VMEM = pl.BlockSpec(memory_space=pltpu.VMEM)
SMEM = pl.BlockSpec(memory_space=pltpu.SMEM)
ANY = pl.BlockSpec(memory_space=pl.ANY)


def split_in_kernel(x):
    high = x.astype(BF16)
    return high, (x - high.astype(F32)).astype(BF16)


def mm(a, b):
    return jnp.dot(a, b, preferred_element_type=F32)


def mm3(a_high, a_low, b_high, b_low):
    left = jnp.concatenate([a_high, a_high, a_low], axis=1)
    right = jnp.concatenate([b_high, b_low, b_high], axis=0)
    return mm(left, right)


def ring_order(count):
    return [0] + list(range(1, count, 2)) + list(range((count - 1) // 2 * 2, 0, -2))


def params(mib, flops, moved):
    return dict(
        compiler_params=pltpu.CompilerParams(vmem_limit_bytes=mib << 20),
        cost_estimate=pl.CostEstimate(flops=flops, bytes_accessed=moved, transcendentals=0),
    )


def invert_call(meta, mine, other, prow, tok_count, rows):
    levels, width = prow.shape
    blocks = width // MB
    systems = blocks * levels
    half = rows // 2
    stride = mine.shape[0] // tok_count

    def kernel(meta_ref, mine_ref, other_ref, prow_ref, u_high, u_low, t_high, t_low, ratio,
               lhs_high, lhs_low, total):
        tok, core = meta_ref[0], meta_ref[1]
        for hop in range(tok_count):
            source = tok ^ hop
            top = hop * stride
            for ref, side in ((mine_ref, core), (other_ref, 1 - core)):
                at = pl.ds(pl.multiple_of(source * rows + side * half, half), half)
                u_high[at, :] = ref[top : top + half, :]
                u_low[at, :] = ref[top + half : top + 2 * half, :]
        row_ids = lax.broadcasted_iota(jnp.int32, (MB, MB), 0)
        col_ids = lax.broadcasted_iota(jnp.int32, (MB, MB), 1)
        eye = jnp.where(row_ids == col_ids, 1.0, 0.0).astype(F32)
        for blk in range(blocks):
            span = slice(blk * MB, (blk + 1) * MB)
            square = u_high[span, span].astype(F32) + u_low[span, span].astype(F32)
            inverse = 1.0 / jnp.sum(square * eye, axis=1, keepdims=True)
            strict = jnp.where(col_ids > row_ids, square, 0.0)
            for lvl in range(levels):
                mask = prow_ref[lvl : lvl + 1, span]
                share = jnp.sum(eye * mask, axis=1, keepdims=True) * inverse
                ratio[span, lvl : lvl + 1] = share
                negated = -(strict * share) * mask
                high, low = split_in_kernel(negated)
                at = blk * levels + lvl
                lhs_high[at, :MB] = high
                lhs_low[at, :MB] = low
                lhs_high[at, MB:] = eye.astype(BF16)
                lhs_low[at, MB:] = jnp.zeros((MB, MB), BF16)
                total[at] = eye
        steps = MB.bit_length() - 1
        for step in range(steps):
            for at in range(systems):
                last = step == steps - 1
                rows_from = slice(MB, None) if last else slice(0, None)
                power = lhs_high[at, :MB]
                both = jnp.concatenate([power, lhs_low[at, :MB]], axis=1)
                first = mm(lhs_high[at, rows_from], both)
                second = mm(lhs_low[at, rows_from], power)
                joined = first[:, :MB] + first[:, MB:] + second
                grown = total[at] + joined[-MB:]
                high, low = split_in_kernel(grown)
                if last:
                    t_high[at] = high
                    t_low[at] = low
                else:
                    total[at] = grown
                    lhs_high[at, MB:] = high
                    lhs_low[at, MB:] = low
                    high, low = split_in_kernel(joined[:MB])
                    lhs_high[at, :MB] = high
                    lhs_low[at, :MB] = low

    return pl.pallas_call(
        kernel,
        out_shape=[jax.ShapeDtypeStruct((width, width), BF16)] * 2
        + [jax.ShapeDtypeStruct((systems, MB, MB), BF16)] * 2
        + [jax.ShapeDtypeStruct((width, levels), F32)],
        in_specs=[SMEM] + [VMEM] * 3,
        out_specs=[VMEM] * 5,
        scratch_shapes=[
            pltpu.VMEM((systems, 2 * MB, MB), BF16),
            pltpu.VMEM((systems, 2 * MB, MB), BF16),
            pltpu.VMEM((systems, MB, MB), F32),
        ],
        name="invert",
        **params(16, 4_000_000_000, 2 << 20),
    )(meta, mine, other, prow)


def back_call(meta, u_high, u_low, t_high, t_low, ratio, pieces, rows):
    width, levels = ratio.shape
    cols = pieces[0].shape[1]
    blocks = width // MB

    def kernel(meta_ref, uh, ul, th, tl, ratio_ref, *refs):
        piece_refs = refs[: len(pieces)]
        k_high, k_low, f_high, f_low = refs[len(pieces) :]
        tok, holds = meta_ref[0], meta_ref[2]
        for hop, ref in enumerate(piece_refs):
            at = pl.ds(pl.multiple_of((tok ^ hop) * rows, rows), rows)
            f_high[at, :] = ref[:rows, :]
            f_low[at, :] = ref[rows:, :]
        for blk in reversed(range(blocks)):
            span = slice(blk * MB, (blk + 1) * MB)
            rest = slice((blk + 1) * MB, width)
            applied = f_high[span, :].astype(F32) + f_low[span, :].astype(F32)
            below = lax.broadcasted_iota(jnp.int32, (MB, cols), 1) < (
                lax.broadcasted_iota(jnp.int32, (MB, cols), 0) + blk * MB
            )
            applied = jnp.where(jnp.logical_and(below, holds == 1), 0.0, applied)
            for lvl in range(levels):
                lanes = slice(lvl * cols, (lvl + 1) * cols)
                target = applied
                if blk < blocks - 1:
                    target = target - mm3(
                        uh[span, rest], ul[span, rest], k_high[rest, lanes], k_low[rest, lanes]
                    )
                high, low = split_in_kernel(target * ratio_ref[span, lvl : lvl + 1])
                at = blk * levels + lvl
                high, low = split_in_kernel(mm3(th[at], tl[at], high, low))
                k_high[span, lanes] = high
                k_low[span, lanes] = low

    return pl.pallas_call(
        kernel,
        out_shape=[jax.ShapeDtypeStruct((width, levels * cols), BF16)] * 2,
        in_specs=[SMEM] + [VMEM] * (5 + len(pieces)),
        out_specs=[VMEM] * 2,
        scratch_shapes=[pltpu.VMEM((width, cols), BF16)] * 2,
        name="back",
        **params(16, 3_000_000_000, 6 << 20),
    )(meta, u_high, u_low, t_high, t_low, ratio, *pieces)


def split_call(inverse_rows):
    rows, width = inverse_rows.shape

    def kernel(x_ref, out_ref):
        high, low = split_in_kernel(x_ref[...])
        out_ref[:rows, :] = high
        out_ref[rows:, :] = low

    return pl.pallas_call(
        kernel,
        out_shape=jax.ShapeDtypeStruct((2 * rows, width), BF16),
        in_specs=[VMEM],
        out_specs=VMEM,
        name="split",
        **params(4, rows * width, 6 * rows * width),
    )(inverse_rows)


def send_call(meta, own_rows, acts, weight, back, low, high, half, row_count):
    tok_rows, width = acts.shape
    rows = own_rows.shape[0] // 2
    depth = tok_rows // row_count
    half_width = width // row_count

    def kernel(meta_ref, own_ref, acts_ref, w_ref, *refs):
        out_ref, sems = refs[-2:]
        core = meta_ref[1]

        def own():
            copies = []

            def copy(source, target):
                copies.append(pltpu.make_async_copy(source, target, sems.at[len(copies)]))
                copies[-1].start()

            if low == 0:
                for part in range(2):
                    top = pl.multiple_of(part * rows + core * half, half)
                    copy(own_ref.at[pl.ds(top, half), :], out_ref.at[pl.ds(part * half, half), :])
            start, stop = max(low, 2 * half), min(high, 2 * half + depth)
            if start < stop:
                left = pl.multiple_of(core * half_width, half_width)
                for i in range(row_count):
                    copy(
                        acts_ref.at[
                            pl.ds(i * depth + start - 2 * half, stop - start),
                            pl.ds(left, half_width),
                        ],
                        out_ref.at[
                            pl.ds(start - low, stop - start), pl.ds(i * half_width, half_width)
                        ],
                    )
            base = 2 * half + depth
            start, stop = max(low, base), min(high, base + weight.shape[0])
            if start < stop:
                copy(
                    w_ref.at[pl.ds(start - base, stop - start), :],
                    out_ref.at[pl.ds(start - low, stop - start), :],
                )
            for item in copies:
                item.wait()

        if back is None:
            own()
        else:
            pl.when(meta_ref[3] == 0)(own)

            @pl.when(meta_ref[3] != 0)
            def _():
                out_ref[...] = refs[0][...]

    extra = [] if back is None else [back]
    return pl.pallas_call(
        kernel,
        out_shape=jax.ShapeDtypeStruct((high - low, width), BF16),
        in_specs=[SMEM] + [ANY] * 3 + [VMEM] * len(extra),
        out_specs=VMEM,
        scratch_shapes=[pltpu.SemaphoreType.DMA((3 + row_count,))],
        name="send",
        **params(2, 0, 4 * (high - low) * width),
    )(meta, own_rows, acts, weight, *extra)


def head_call(meta, own_rows, options, half):
    rows, width = own_rows.shape[0] // 2, own_rows.shape[1]

    def kernel(meta_ref, own_ref, *refs):
        out_ref = refs[-1]

        @pl.when(meta_ref[3] == 0)
        def _():
            for part in range(2):
                top = pl.multiple_of(part * rows + meta_ref[1] * half, half)
                out_ref[part * half : (part + 1) * half, :] = own_ref[pl.ds(top, half), :]

        for j in range(len(options)):

            @pl.when(meta_ref[3] == j + 1)
            def _():
                out_ref[...] = refs[j][: 2 * half, :]

    return pl.pallas_call(
        kernel,
        out_shape=jax.ShapeDtypeStruct((2 * half, width), BF16),
        in_specs=[SMEM] + [VMEM] * (1 + len(options)),
        out_specs=VMEM,
        name="head",
        **params(2, 0, 4 * half * width),
    )(meta, own_rows, *options)


def join_call(items):
    rows, width = items[0].shape

    def kernel(*refs):
        for i in range(len(items)):
            refs[-1][i * rows : (i + 1) * rows, :] = refs[i][...]

    return pl.pallas_call(
        kernel,
        out_shape=jax.ShapeDtypeStruct((len(items) * rows, width), BF16),
        in_specs=[VMEM] * len(items),
        out_specs=VMEM,
        name="join",
        **params(4, 0, 4 * len(items) * rows * width),
    )(*items)


def pick_rows(refs, segments, hops, distance, picked):
    for j in range(hops):

        @pl.when(distance == j + 1)
        def _():
            at = 0
            for i, (_, low, high) in enumerate(segments):
                picked[at : at + high - low, :] = refs[i * hops + j][low:high, :]
                at += high - low


def hessian_call(meta, segments, options, acts, scale, tok_count, row_count, factor_rows):
    tok_rows, width = acts.shape
    half_width = width // row_count
    hops = len(options[0])
    depth = tok_rows // row_count
    dims = (((0,), (0,)), ((), ()))

    def kernel(meta_ref, *refs):
        count = len(segments) * hops
        acts_ref = refs[count]
        sent = refs[count + 1 : count + 1 + tok_count]
        picked, part = refs[count + 1 + tok_count :]
        tok = meta_ref[0]
        pick_rows(refs, segments, hops, meta_ref[3], picked)

        @pl.when(meta_ref[3] == 0)
        def _():
            left = pl.multiple_of(meta_ref[1] * half_width, half_width)
            for i in range(row_count):
                picked[:, i * half_width : (i + 1) * half_width] = acts_ref[
                    i * depth : (i + 1) * depth, pl.ds(left, half_width)
                ]

        product = None
        for i in range(row_count):
            term = lax.dot_general(
                picked[:, i * half_width : (i + 1) * half_width],
                acts_ref[i * depth : (i + 1) * depth, :],
                dims,
                preferred_element_type=F32,
            )
            product = term if product is None else product + term
        part[...] = product * scale
        for hop in range(tok_count):
            place = tok ^ hop
            top = pl.multiple_of(place // row_count * factor_rows, factor_rows)
            left = pl.multiple_of(place % row_count * half_width, half_width)
            sent[hop][...] = part[pl.ds(top, factor_rows), pl.ds(left, half_width)]

    flat = [array for item in options for array in item]
    return pl.pallas_call(
        kernel,
        out_shape=[jax.ShapeDtypeStruct((factor_rows, half_width), F32)] * tok_count,
        in_specs=[SMEM] + [VMEM] * (len(flat) + 1),
        out_specs=[VMEM] * tok_count,
        scratch_shapes=[pltpu.VMEM((depth, width), BF16), pltpu.VMEM((half_width, width), F32)],
        name="hess",
        **params(12, 2 * tok_rows * half_width * width, 3 << 20),
    )(meta, *flat, acts)


def update_call(meta, segments, options, weight, k_high, k_low, keep, result, start):
    levels, cols = keep.shape
    out_rows = weight.shape[0]
    width = k_high.shape[0]
    hops = len(options[0])
    tall = sum(high - low for _, low, high in segments)
    flat = [array for item in options for array in item]

    def kernel(meta_ref, *refs):
        count = len(flat)
        w_ref, high_ref, low_ref, keep_ref = refs[count : count + 4]
        out_ref, picked, ready, own, sems = refs[-5:]
        fetch = pltpu.make_async_copy(w_ref.at[pl.ds(start, tall), :], own, sems.at[levels])
        fetch.start()
        pick_rows(refs, segments, hops, meta_ref[3], picked)
        fetch.wait()

        @pl.when(meta_ref[3] == 0)
        def _():
            picked[...] = own[...]

        panel = picked[...]
        copies = []
        for lvl in range(levels):
            lanes = slice(lvl * cols, (lvl + 1) * cols)
            change = mm(panel, high_ref[:, lanes]) + mm(panel, low_ref[:, lanes])
            value = own[...].astype(F32) - change
            ready[lvl] = (value * keep_ref[lvl : lvl + 1, :]).astype(BF16)
            copy = pltpu.make_async_copy(
                ready.at[lvl], out_ref.at[lvl, pl.ds(start, tall), :], sems.at[lvl]
            )
            copy.start()
            copies.append(copy)
        for copy in copies:
            copy.wait()

    operands = [meta] + flat + [weight, k_high, k_low, keep]
    in_specs = [SMEM] + [VMEM] * len(flat) + [ANY] + [VMEM] * 3
    aliases = {}
    if result is not None:
        aliases = {len(operands): 0}
        operands.append(result)
        in_specs.append(ANY)
    return pl.pallas_call(
        kernel,
        out_shape=jax.ShapeDtypeStruct((levels, out_rows, cols), BF16),
        in_specs=in_specs,
        out_specs=ANY,
        scratch_shapes=[
            pltpu.VMEM((tall, width), BF16),
            pltpu.VMEM((levels, tall, cols), BF16),
            pltpu.VMEM((tall, cols), BF16),
            pltpu.SemaphoreType.DMA((levels + 1,)),
        ],
        input_output_aliases=aliases,
        **params(14, 4 * tall * width * levels * cols, 4 << 20),
    )(*operands)


def on_device(activations, weight, inverse_rows, prune_masks, panel_order):
    col_count = lax.axis_size("col")
    tok_count = lax.axis_size("tok")
    row_count = lax.axis_size("row")
    tok_rows, block_width = activations.shape
    out_rows = weight.shape[0]
    factor_rows = inverse_rows.shape[0]
    root = panel_order[0] // (block_width // MB)
    col, tok, core = lax.axis_index("col"), lax.axis_index("tok"), lax.axis_index("row")

    order = ring_order(col_count)
    ring = [(order[i], order[(i + 1) % col_count]) for i in range(col_count)]
    spot = jnp.array([order.index(i) for i in range(col_count)], jnp.int32)
    distance = lax.rem(spot[col] - spot[root] + col_count, col_count)
    holds = (col == root).astype(jnp.int32)
    meta = jnp.stack([tok, core, holds, distance]).astype(jnp.int32)

    def tok_gather(item):
        return [item] + [
            lax.ppermute(item, "tok", [(i ^ hop, i) for i in range(tok_count)])
            for hop in range(1, tok_count)
        ]

    half = factor_rows // row_count
    own_rows = split_call(inverse_rows)
    bounds = [0]
    for rows in (2 * half, tok_rows // row_count, out_rows):
        bounds.append(bounds[-1] + rows)
    chunk = -(-bounds[-1] // (CHUNKS * 16)) * 16
    chunk_count = -(-bounds[-1] // chunk)

    got = []
    for k in range(chunk_count + DELAY * (col_count - 2)):
        send = got[k - DELAY] if k >= DELAY else None
        if k < chunk_count:
            send = send_call(
                meta, own_rows, activations, weight, send, k * chunk, (k + 1) * chunk, half,
                row_count,
            )
        got.append(lax.ppermute(send, "col", ring))

    def options_of(index):
        return [got[index + DELAY * (j - 1)] for j in range(1, col_count)]

    def segments_of(low, high):
        out = []
        while low < high:
            index = low // chunk
            stop = min(high, (index + 1) * chunk)
            out.append((index, low - index * chunk, stop - index * chunk))
            low = stop
        return out

    pieces_f = tok_gather(own_rows)

    head = head_call(meta, own_rows, options_of(0), half)
    gathered = tok_gather(head)
    mine_u = join_call(gathered)
    other_u = lax.ppermute(mine_u, "row", [(0, 1), (1, 0)])

    level_masks = lax.dynamic_slice_in_dim(
        prune_masks, root * block_width, block_width, 1
    ).astype(F32)
    inverted = invert_call(
        meta, mine_u, other_u, level_masks, tok_count, factor_rows
    )
    k_high, k_low = back_call(meta, *inverted, pieces_f, factor_rows)

    segments = segments_of(bounds[1], bounds[2])
    sent = hessian_call(
        meta, segments, [options_of(s[0]) for s in segments], activations,
        2.0 / (tok_rows * tok_count), tok_count, row_count, factor_rows,
    )
    per_core = tok_count // row_count
    hessian = None
    for hop in range(tok_count):
        pairs = [
            (
                t * row_count + r,
                (per_core * r + (t ^ hop) // row_count) * row_count + (t ^ hop) % row_count,
            )
            for t in range(tok_count)
            for r in range(row_count)
        ]
        part = lax.ppermute(sent[hop], ("tok", "row"), pairs)
        hessian = part if hessian is None else hessian + part

    keep = jnp.where(holds == 1, 1.0 - level_masks, jnp.ones_like(level_masks))
    cut = max(bounds[2], (chunk_count - LAST) * chunk)
    result = None
    for low, high in ((bounds[2], cut), (cut, bounds[3])):
        if low < high:
            segments = segments_of(low, high)
            result = update_call(
                meta, segments, [options_of(s[0]) for s in segments], weight, k_high, k_low,
                keep, result, low - bounds[2],
            )
    return hessian, result


def solution(mesh):
    in_specs = (P("tok", "col"), P(("tok", "row"), "col"), P("tok", "col"), P(), P())
    out_specs = (P("tok", ("col", "row")), P(None, ("tok", "row"), "col"))

    return jax.shard_map(
        on_device, mesh=mesh, in_specs=in_specs, out_specs=out_specs, check_vma=False
    )
```
